1024 devices in a mesh: gx: 16 (over x, z_lo), gz: 64 (over z_hi, y, core).
Axes of the slice: x: 4, y: 8, z: 16 (z_hi: 4, z_lo: 4; z = z_hi * 4 + z_lo), core: 2. Of those that a mesh axis runs over, the one named last changes fastest.
Arguments:
- source: float32 [256, 16, 8192], P('gx', None, 'gz'), may hold values from -14 to 14
- previous: float32 [256, 16, 8192], P('gx', None, 'gz'), may hold values from -6 to 6
- coefficients: float32 [3, 32, 2, 1024], P(None, 'gx', None, 'gz'), may hold values from 0.3 to 3
- stiffness: float32 [8, 8], replicated, may hold values from -0.2 to 2.5, as said below
- fdm_vectors: float32 [8, 8], replicated, may hold values from -0.1 to 1.2
- fdm_values: float32 [8], replicated, may hold values from 0.1 to 10
- coarse_inverse: float32 [2048, 2048], P(('gx', 'gz')), may hold values from -0.004 to 0.008, as said below
- vertex_map: int32 [8, 32, 2, 1024], P(None, 'gx', None, 'gz'), may hold values from 0 to 2047, as said below
Outputs:
- new_solution: float32 [256, 16, 8192], P('gx', None, 'gz')
- new_residual: float32 [256, 16, 8192], P('gx', None, 'gz')
The draws below stay inside these ranges and needn't reach their ends.
Inputs may be any that keep to these rules, and one draw needn't show every extreme that they name: stiffness is symmetric. coarse_inverse is symmetric. `vertex_map`: corners of elements that meet at one grid vertex carry the same number; each number labels the vertices of one aligned block of 2 x 3 x 8 grid vertices along the three dimensions; every number occurs.
All inputs are finite; a program needn't handle non-finite values.
Results may differ from the reference program's by a relative error of at most 0.00012.
Values sent between devices are 32-bit elements; how exact they have to be, the bound alone decides.
A program may use at most 32 MiB of HBM per device.

```python
import math
import jax
import jax.numpy as jnp
from jax import lax

NODES = 8
WALL_LAYERS = 2
STREAM_ELEMENTS = 32
SPAN_ELEMENTS = 1024
NXN = 256
NYN = 16
NZN = 8192
NV = 2048


def draw_source(key, part):
    key_values = jax.random.fold_in(key, 0)
    along_x = 0.5 + jnp.arange(NXN, dtype=jnp.float32) / NXN
    along_z = 0.5 + jnp.arange(NZN, dtype=jnp.float32) / NZN
    ramp = along_x[:, None, None] * along_z[None, None, :]
    rough = jnp.clip(jax.random.normal(key_values, (NXN, NYN, NZN), jnp.float32), -6.0, 6.0)
    return ramp * rough


def draw_stiffness(key, part):
    key_diag, key_off = jax.random.split(key)
    offdiag = jax.random.uniform(key_off, (NODES, NODES), jnp.float32, -0.2, 0.2)
    offdiag = (offdiag + offdiag.T) / 2.0
    diagonal = jax.random.uniform(key_diag, (NODES,), jnp.float32, 1.5, 2.5)
    return jnp.where(jnp.eye(NODES, dtype=bool), jnp.diag(diagonal), offdiag)


def draw_fdm_vectors(key, part):
    key_diag, key_off = jax.random.split(key)
    offdiag = jax.random.uniform(key_off, (NODES, NODES), jnp.float32, -0.1, 0.1)
    diagonal = jax.random.uniform(key_diag, (NODES,), jnp.float32, 0.8, 1.2)
    return jnp.where(jnp.eye(NODES, dtype=bool), jnp.diag(diagonal), offdiag)


def draw_coarse_inverse(key, part):
    key_diag, key_off = jax.random.split(key)
    offdiag = jax.random.uniform(key_off, (NV, NV), jnp.float32, -1.0, 1.0)
    offdiag = (offdiag + offdiag.T) * (0.45 / NV)
    diagonal = jax.random.uniform(key_diag, (NV,), jnp.float32, 1.0, 2.0)
    return 0.004 * jnp.where(jnp.eye(NV, dtype=bool), jnp.diag(diagonal), offdiag)


def draw_vertex_map(key, part):
    groups_y = (WALL_LAYERS + 1) // 3
    spanwise_groups = SPAN_ELEMENTS // 8
    labels = jax.random.permutation(key, NV).astype(jnp.int32)
    corner_point = jnp.arange(8, dtype=jnp.int32).reshape(8, 1, 1, 1)
    vertex_x = (jnp.arange(STREAM_ELEMENTS, dtype=jnp.int32).reshape(1, STREAM_ELEMENTS, 1, 1) + corner_point // 4) % STREAM_ELEMENTS
    vertex_y = jnp.arange(WALL_LAYERS, dtype=jnp.int32).reshape(1, 1, WALL_LAYERS, 1) + corner_point // 2 % 2
    spanwise_vertex = (jnp.arange(SPAN_ELEMENTS, dtype=jnp.int32).reshape(1, 1, 1, SPAN_ELEMENTS) + corner_point % 2) % SPAN_ELEMENTS
    group = vertex_x // 2 * (groups_y * spanwise_groups) + vertex_y // 3 * spanwise_groups + spanwise_vertex // 8
    return labels[group].astype(jnp.int32)


def block_scale(stream_key, extent, pieces, least, top_value):
    level, own = 1.0, jax.random.fold_in(stream_key, 6)
    for dim, parts in pieces:
        steps = jnp.exp(jax.random.uniform(jax.random.fold_in(own, dim), (parts,), jnp.float32, least / len(pieces), top_value / len(pieces)))
        level = level * jnp.repeat(steps, extent[dim] // parts).reshape([-1 if axis == dim else 1 for axis in range(len(extent))])
    return level


def normal_values(rng, shape, scale, bound, pieces=(), kind=jnp.bfloat16):
    loudness = block_scale(rng, shape, pieces, -0.22, 0.18) if pieces else 1.0
    values = jax.random.normal(rng, shape, jnp.float32) * scale * loudness
    return jnp.minimum(jnp.maximum(values, -bound), bound).astype(kind)


def setup_inputs(seed: int = 0) -> dict:
    splits = jax.random.split(jax.random.key(seed), 9)
    return {
        "source": draw_source(jax.random.fold_in(splits[8], 71), 0),
        "previous": normal_values(splits[1], (NXN, NYN, NZN), 1.0, 6.0, ((0, 16), (2, 64)), jnp.float32),
        "coefficients": jnp.clip(jnp.exp(math.log(3.0) - 2.3025851 * jax.random.uniform(splits[2], (3, STREAM_ELEMENTS, WALL_LAYERS, SPAN_ELEMENTS), jnp.float32) ** block_scale(splits[2], (3, STREAM_ELEMENTS, WALL_LAYERS, SPAN_ELEMENTS), ((1, 16), (3, 64)), -0.2, 0.2)), 0.3, 3.0),
        "stiffness": draw_stiffness(jax.random.fold_in(splits[8], 71), 0),
        "fdm_vectors": draw_fdm_vectors(jax.random.fold_in(splits[8], 71), 0),
        "fdm_values": jnp.clip(jnp.exp(jax.random.uniform(splits[5], (NODES,), jnp.float32, math.log(0.1), math.log(10.0))), 0.1, 10.0),
        "coarse_inverse": draw_coarse_inverse(jax.random.fold_in(splits[8], 71), 0),
        "vertex_map": draw_vertex_map(jax.random.fold_in(splits[8], 71), 0),
    }


GLL_POINTS = [-1.0, -0.8717401485096066, -0.5917001814331423, -0.2092992179024789, 0.2092992179024789, 0.5917001814331423, 0.8717401485096066, 1.0]
GLL_WEIGHTS = [0.03571428571428571, 0.21070422714350603, 0.34112269248350436, 0.4124587946587038, 0.4124587946587038, 0.34112269248350436, 0.21070422714350603, 0.03571428571428571]


def node_weights(length):
    return jnp.tile(jnp.array(GLL_WEIGHTS, dtype=jnp.float32), length // 8)


def contract_axis(values, matrix, axis_number):
    layout = values.shape
    length = layout[axis_number]
    split = values.reshape(layout[:axis_number] + (length // 8, 8) + layout[axis_number + 1:])
    moved = jnp.moveaxis(split, axis_number + 1, -1)
    result = jnp.einsum('...p,ip->...i', moved, matrix, precision=lax.Precision.HIGHEST)
    return jnp.moveaxis(result, -1, axis_number + 1).reshape(layout)


def pair_sum(values, axis_number, periodic):
    length = values.shape[axis_number]
    if periodic:
        upper = jnp.roll(values, -1, axis=axis_number)
        lower = jnp.roll(values, 1, axis=axis_number)
    else:
        widths = [(0, 0), (0, 0), (0, 0)]
        widths[axis_number] = (1, 1)
        padded = jnp.pad(values, widths)
        upper = lax.slice_in_dim(padded, 2, length + 2, axis=axis_number)
        lower = lax.slice_in_dim(padded, 0, length, axis=axis_number)
    layout = [1, 1, 1]
    layout[axis_number] = length
    position = (jnp.arange(length) % 8).reshape(layout)
    return values + jnp.where(position == 7, upper, 0.0) + jnp.where(position == 0, lower, 0.0)


def assemble(values):
    values = pair_sum(values, 0, True)
    values = pair_sum(values, 1, False)
    return pair_sum(values, 2, True)


def spread(layer):
    return jnp.repeat(jnp.repeat(jnp.repeat(layer, 8, axis=0), 8, axis=1), 8, axis=2)


def apply_operator(values, spreads, stiffness):
    weight_x = node_weights(values.shape[0])[:, None, None]
    weight_y = node_weights(values.shape[1])[None, :, None]
    weight_z = node_weights(values.shape[2])[None, None, :]
    result = spreads[0] * contract_axis(values, stiffness, 0) * weight_y * weight_z
    result = result + spreads[1] * contract_axis(values, stiffness, 1) * weight_x * weight_z
    return result + spreads[2] * contract_axis(values, stiffness, 2) * weight_x * weight_y


def local_solve(values, spreads, vectors, eigen):
    moved = contract_axis(values, vectors.T, 0)
    moved = contract_axis(moved, vectors.T, 1)
    moved = contract_axis(moved, vectors.T, 2)
    lam_x = jnp.tile(eigen, values.shape[0] // 8)[:, None, None]
    lam_y = jnp.tile(eigen, values.shape[1] // 8)[None, :, None]
    lam_z = jnp.tile(eigen, values.shape[2] // 8)[None, None, :]
    moved = moved / (spreads[0] * lam_x + spreads[1] * lam_y + spreads[2] * lam_z)
    moved = contract_axis(moved, vectors, 0)
    moved = contract_axis(moved, vectors, 1)
    return contract_axis(moved, vectors, 2)


def reference(source, previous, coefficients, stiffness, fdm_vectors, fdm_values, coarse_inverse, vertex_map):
    rows_x, rows_y, spanwise_rows = source.shape
    elements_x, elements_y, elements_z = rows_x // 8, rows_y // 8, spanwise_rows // 8
    count_coarse = coarse_inverse.shape[0]
    copies = assemble(jnp.ones_like(source))
    keep = (jnp.arange(rows_y) < rows_y - 1).astype(source.dtype).reshape(1, rows_y, 1)
    spreads = [spread(coefficients[component]) for component in range(3)]
    start = keep * assemble(previous) / copies
    residual = keep * assemble(source - apply_operator(start, spreads, stiffness))
    local_part = local_solve(residual, spreads, fdm_vectors, fdm_values)
    points = jnp.array(GLL_POINTS, dtype=jnp.float32)
    basis = jnp.stack([(1.0 - points) / 2.0, (1.0 + points) / 2.0])
    weighted = (residual / copies).reshape(elements_x, 8, elements_y, 8, elements_z, 8)
    corner_sums = jnp.einsum('xi,yj,zk,aibjek->axbyez', basis, basis, basis, weighted, precision=lax.Precision.HIGHEST)
    corner_sums = corner_sums.transpose(1, 3, 5, 0, 2, 4).reshape(8, elements_x, elements_y, elements_z)
    coarse_rhs = jax.ops.segment_sum(corner_sums.reshape(-1), vertex_map.reshape(-1).astype(jnp.int32), num_segments=count_coarse)
    coarse_values = jnp.dot(coarse_inverse, coarse_rhs, precision=lax.Precision.HIGHEST)
    picked = coarse_values[vertex_map.astype(jnp.int32)].reshape(2, 2, 2, elements_x, elements_y, elements_z)
    picked = picked.transpose(3, 0, 4, 1, 5, 2)
    coarse_part = jnp.einsum('axbyez,xi,yj,zk->aibjek', picked, basis, basis, basis, precision=lax.Precision.HIGHEST)
    coarse_part = coarse_part.reshape(rows_x, rows_y, spanwise_rows)
    precond = keep * (assemble(local_part) + coarse_part)
    numerator = jnp.sum(residual * precond / copies)
    image = keep * assemble(apply_operator(precond, spreads, stiffness))
    denominator = jnp.sum(precond * image / copies)
    alpha = numerator / denominator
    return start + alpha * precond, residual - alpha * image
```

```python
import functools

import jax
import jax.numpy as jnp
from jax import lax
from jax.experimental import pallas as pl
from jax.experimental.pallas import tpu as pltpu
from jax.sharding import PartitionSpec as P

MESH = pl.DeviceIdType.MESH
HIGHEST = lax.Precision.HIGHEST

GLL_POINTS = [
    -1.0,
    -0.8717401485096066,
    -0.5917001814331423,
    -0.2092992179024789,
    0.2092992179024789,
    0.5917001814331423,
    0.8717401485096066,
    1.0,
]
GLL_WEIGHTS = [
    0.03571428571428571,
    0.21070422714350603,
    0.34112269248350435,
    0.4124587946587038,
    0.4124587946587038,
    0.34112269248350435,
    0.21070422714350603,
    0.03571428571428571,
]
PHI_0 = [(1.0 - s) / 2.0 for s in GLL_POINTS]
PHI_1 = [(1.0 + s) / 2.0 for s in GLL_POINTS]

FIELD = (2, 8, 2, 8, 128)
ROWS = (256, 128)


def iota(shape, dim):
    return lax.broadcasted_iota(jnp.int32, shape, dim)


def table(index, values):
    result = jnp.full(index.shape, values[0], jnp.float32)
    for i in range(1, len(values)):
        result = jnp.where(index == i, values[i], result)
    return result


def tile_kernel(
    shape,
    source,
    previous,
    coefficients,
    stiffness,
    vectors,
    eigen,
    coarse,
    labels,
    out_solution,
    out_residual,
    x_send,
    x_recv,
    z_send,
    z_recv,
    row_send,
    label_rows,
    rhs_rows,
    line_rows,
    value_rows,
    sum_rows,
    total_rows,
    coarse_rows,
    onehot,
    x_sems,
    z_sems,
    x_sent,
    z_sent,
    row_sems,
    row_sent,
):
    XS, ZL, ZH, YC = shape
    Q, NZ = XS * YC, ZL * ZH
    gx, gz = lax.axis_index("gx"), lax.axis_index("gz")
    x, zl = lax.div(gx, ZL), lax.rem(gx, ZL)
    zh, yc = lax.div(gz, YC), lax.rem(gz, YC)
    q, zi = x * YC + yc, zh * ZL + zl
    GX, GZ = XS * ZL, ZH * YC
    left, right = lax.rem(gx + GX - 1, GX), lax.rem(gx + 1, GX)
    down, up = lax.rem(gz + GZ - 1, GZ), lax.rem(gz + 1, GZ)

    def plane_peer(k):
        other = lax.rem(q + k, Q)
        return {"gx": lax.div(other, YC) * ZL + zl, "gz": zh * YC + lax.rem(other, YC)}

    def line_peer(k):
        other = lax.rem(zi + k, NZ)
        return {"gx": x * ZL + lax.rem(other, ZL), "gz": lax.div(other, ZL) * YC + yc}

    neighbours = [
        (left, gz),
        (right, gz),
        (gx, down),
        (gx, up),
        (left, down),
        (left, up),
        (right, down),
        (right, up),
    ]

    barrier = pltpu.get_barrier_semaphore()
    for a, b in neighbours:
        pl.semaphore_signal(barrier, inc=1, device_id={"gx": a, "gz": b}, device_id_type=MESH)

    def greet_line(k, carry):
        pl.semaphore_signal(barrier, inc=1, device_id=line_peer(k), device_id_type=MESH)
        return carry

    def greet_plane(k, carry):
        pl.semaphore_signal(barrier, inc=1, device_id=plane_peer(k), device_id_type=MESH)
        return carry

    lax.fori_loop(1, NZ, greet_line, 0)
    lax.fori_loop(1, Q, greet_plane, 0)

    lane8 = iota((8, 128), 1)
    sub8 = iota((8, 128), 0)
    lane1 = iota((1, 128), 1)
    inner = lane8 & 7
    inner1 = lane1 & 7
    element1 = lane1 >> 3
    weight_z = table(inner, GLL_WEIGHTS)
    weight_y = table(sub8, GLL_WEIGHTS)
    edge_z = (inner == 0) | (inner == 7)
    half_z = jnp.where(edge_z, 0.5, 1.0)
    inv_yz = [jnp.where(sub8 == 7, 0.5, 1.0) * half_z, jnp.where(sub8 == 0, 0.5, 1.0) * half_z]
    keep_y = jnp.where(sub8 == 7, 0.0, 1.0)
    inv_x = [0.5, 1.0, 1.0, 1.0, 1.0, 1.0, 1.0, 0.5]

    def join(parts):
        return jnp.stack(
            [jnp.stack([jnp.stack(parts[a][i]) for i in range(8)]) for a in range(2)]
        )

    spread_matrix = ((iota((16, 128), 1) >> 3) == iota((16, 128), 0)).astype(jnp.float32)
    spreads = []
    for c in range(3):
        per_x = []
        for a in range(2):
            rows = jnp.dot(
                coefficients[c, a], spread_matrix, precision=HIGHEST, preferred_element_type=jnp.float32
            )
            per_x.append([jnp.broadcast_to(rows[b : b + 1], (8, 128)) for b in range(2)])
        spreads.append(per_x)

    def columns(matrix, transposed):
        return [
            table(sub8, [matrix[p, j] if transposed else matrix[j, p] for j in range(8)]) for p in range(8)
        ]

    def block_matrix(matrix_columns):
        tile = matrix_columns[0]
        for p in range(1, 8):
            tile = jnp.where(inner == p, matrix_columns[p], tile)
        full = jnp.concatenate([tile] * 16, axis=0)
        same = (iota((128, 128), 0) >> 3) == (iota((128, 128), 1) >> 3)
        return jnp.where(same, full, 0.0)

    stiff_columns = columns(stiffness, False)
    vector_columns = columns(vectors, False)
    vector_rows = columns(vectors, True)
    stiff_z = block_matrix(columns(stiffness, True))
    forward_z = block_matrix(vector_columns)
    backward_z = block_matrix(vector_rows)

    def along_x(v, entry):
        return jnp.stack(
            [
                jnp.stack([functools.reduce(jnp.add, [entry(i, p) * v[a, p] for p in range(8)]) for i in range(8)])
                for a in range(2)
            ]
        )

    def along_y(v, cols):
        return functools.reduce(
            jnp.add, [cols[p] * jnp.broadcast_to(v[:, :, :, p : p + 1, :], FIELD) for p in range(8)]
        )

    def along_z(v, matrix):
        return jnp.dot(
            v.reshape(ROWS), matrix, precision=HIGHEST, preferred_element_type=jnp.float32
        ).reshape(FIELD)

    factor_x = [[spreads[0][a][b] * weight_y * weight_z for b in range(2)] for a in range(2)]
    factor_y = [[spreads[1][a][b] * weight_z for b in range(2)] for a in range(2)]
    factor_z = [[spreads[2][a][b] * weight_y for b in range(2)] for a in range(2)]

    def apply_operator(v):
        vx = along_x(v, lambda i, p: stiffness[i, p])
        vy = along_y(v, stiff_columns)
        vz = along_z(v, stiff_z)
        return join(
            [
                [
                    [
                        factor_x[a][b] * vx[a, i, b]
                        + GLL_WEIGHTS[i] * (factor_y[a][b] * vy[a, i, b] + factor_z[a][b] * vz[a, i, b])
                        for b in range(2)
                    ]
                    for i in range(8)
                ]
                for a in range(2)
            ]
        )

    def local_solve(v):
        t = along_x(v, lambda i, p: vectors[p, i])
        t = along_y(t, vector_rows)
        t = along_z(t, forward_z)
        lam_y = table(sub8, [eigen[k] for k in range(8)])
        lam_z = table(inner, [eigen[k] for k in range(8)])
        rest = [[spreads[1][a][b] * lam_y + spreads[2][a][b] * lam_z for b in range(2)] for a in range(2)]
        t = join(
            [
                [[t[a, i, b] / (spreads[0][a][b] * eigen[i] + rest[a][b]) for b in range(2)] for i in range(8)]
                for a in range(2)
            ]
        )
        t = along_x(t, lambda i, p: vectors[i, p])
        t = along_y(t, vector_columns)
        return along_z(t, backward_z)

    low_z = (inner == 0) & (lane8 > 0)
    high_z = (inner == 7) & (lane8 < 127)

    def add_inside(v):
        flat = v.reshape(ROWS)
        after = pltpu.roll(flat, 127, 1).reshape(FIELD)
        before = pltpu.roll(flat, 1, 1).reshape(FIELD)
        v = v + jnp.where(high_z, after, 0.0) + jnp.where(low_z, before, 0.0)
        first, second = v[:, :, 0], v[:, :, 1]
        to_first = jnp.broadcast_to(second[:, :, 0:1, :], (2, 8, 8, 128))
        to_second = jnp.broadcast_to(first[:, :, 7:8, :], (2, 8, 8, 128))
        first = first + jnp.where(sub8 == 7, to_first, 0.0)
        second = second + jnp.where(sub8 == 0, to_second, 0.0)
        v = jnp.stack([first, second], axis=2)
        seam = v[0, 7] + v[1, 0]
        return jnp.stack(
            [
                jnp.concatenate([v[0, :7], seam[None]], axis=0),
                jnp.concatenate([seam[None], v[1, 1:]], axis=0),
            ]
        )

    picker = jnp.where(((sub8 == 0) & (lane8 == 0)) | ((sub8 == 1) & (lane8 == 127)), 1.0, 0.0)
    wide = iota((8, 256), 1)

    def send_faces(n, v):
        x_send[n, 0] = v[0, 0].reshape(16, 128)
        x_send[n, 1] = v[1, 7].reshape(16, 128)
        faces = lax.dot_general(
            picker,
            v.reshape(ROWS),
            (((1,), (1,)), ((), ())),
            precision=HIGHEST,
            preferred_element_type=jnp.float32,
        )
        plus = jnp.where(wide < 16, pltpu.roll(faces, 16, 1), 0.0)
        minus = jnp.where(wide >= 240, pltpu.roll(faces, 240, 1), 0.0)
        for k, value in enumerate((faces, plus, minus)):
            z_send[n, 2 * k] = value[0:1]
            z_send[n, 2 * k + 1] = value[1:2]
        plan = [
            (0, 3, gx, down),
            (1, 0, gx, up),
            (2, 4, right, down),
            (3, 1, right, up),
            (4, 5, left, down),
            (5, 2, left, up),
        ]
        for src, dst, a, b in plan:
            pltpu.make_async_remote_copy(
                src_ref=z_send.at[n, src],
                dst_ref=z_recv.at[n, dst],
                send_sem=z_sent.at[n, src],
                recv_sem=z_sems.at[n, dst],
                device_id={"gx": a, "gz": b},
                device_id_type=MESH,
            ).start()
        for src, dst, a in ((0, 1, left), (1, 0, right)):
            pltpu.make_async_remote_copy(
                src_ref=x_send.at[n, src],
                dst_ref=x_recv.at[n, dst],
                send_sem=x_sent.at[n, src],
                recv_sem=x_sems.at[n, dst],
                device_id={"gx": a, "gz": gz},
                device_id_type=MESH,
            ).start()

    def receive_faces(n, v):
        for s in range(2):
            pltpu.make_async_copy(x_recv.at[n, s], x_recv.at[n, s], x_sems.at[n, s]).wait()
        for s in range(6):
            pltpu.make_async_copy(z_recv.at[n, s], z_recv.at[n, s], z_sems.at[n, s]).wait()
        low = z_recv[n, 0] + z_recv[n, 1] + z_recv[n, 2]
        high = z_recv[n, 3] + z_recv[n, 4] + z_recv[n, 5]
        sub = iota((8, 256), 0)
        both = jnp.where(sub == 0, jnp.broadcast_to(low, (8, 256)), 0.0)
        both = jnp.where(sub == 1, jnp.broadcast_to(high, (8, 256)), both)
        add = lax.dot_general(
            both, picker, (((0,), (0,)), ((), ())), precision=HIGHEST, preferred_element_type=jnp.float32
        ).reshape(FIELD)
        v = v + add
        top = v[0, 0] + x_recv[n, 0].reshape(2, 8, 128)
        bottom = v[1, 7] + x_recv[n, 1].reshape(2, 8, 128)
        return jnp.stack(
            [
                jnp.concatenate([top[None], v[0, 1:]], axis=0),
                jnp.concatenate([v[1, :7], bottom[None]], axis=0),
            ]
        )

    def masked(v):
        return jnp.stack([v[:, :, 0], v[:, :, 1] * keep_y], axis=2)

    def over_copies(v):
        return join(
            [[[v[a, i, b] * (inv_yz[b] * inv_x[i]) for b in range(2)] for i in range(8)] for a in range(2)]
        )

    def total(v):
        rows = jnp.sum(v.reshape(32, 8, 128), axis=0)
        return jnp.sum(jnp.sum(rows, axis=1, keepdims=True), axis=0, keepdims=True)

    def send_rows(n, src, rows, slot, count, peer):
        pltpu.make_async_copy(src, rows.at[slot], row_sems.at[n]).start()

        def step(k, carry):
            pltpu.make_async_remote_copy(
                src_ref=src,
                dst_ref=rows.at[slot],
                send_sem=row_sent.at[n],
                recv_sem=row_sems.at[n],
                device_id=peer(k),
                device_id_type=MESH,
            ).start()
            return carry

        lax.fori_loop(1, count, step, 0)

    def wait_rows(n, rows):
        pltpu.make_async_copy(rows, rows, row_sems.at[n]).wait()

    def wait_sent(n, rows, count):
        part = rows.at[pl.ds(0, count - 1)]
        pltpu.make_async_copy(part, part, row_sent.at[n]).wait()

    ramp_0, ramp_1 = table(inner1, PHI_0), table(inner1, PHI_1)
    one, zero = jnp.ones((1, 128), jnp.float32), jnp.zeros((1, 128), jnp.float32)
    block_z = [
        jnp.where(element1 < 7, one, jnp.where(element1 == 7, ramp_0, zero)),
        jnp.where(
            element1 == 7,
            ramp_1,
            jnp.where(element1 == 15, ramp_0, jnp.where(element1 > 7, one, zero)),
        ),
        jnp.where(element1 == 15, ramp_1, zero),
    ]
    own_labels = [
        labels[0, 0, 0, 0],
        labels[0, 0, 0, 8],
        labels[1, 0, 0, 15],
        labels[4, 1, 0, 0],
        labels[4, 1, 0, 8],
        labels[5, 1, 0, 15],
    ]
    GROUP = min(16, Q)
    GROUPS = Q // GROUP
    slot_base = 8 * lax.rem(q, GROUP)

    label_row = jnp.zeros((1, 128), jnp.float32)
    for s in range(6):
        label_row = jnp.where(lane1 == slot_base + s, own_labels[s].astype(jnp.float32), label_row)
    row_send[0] = label_row

    started = add_inside(previous[...].reshape(FIELD))

    pl.semaphore_wait(barrier, 8 + (NZ - 1) + (Q - 1))

    send_faces(0, started)
    send_rows(0, row_send.at[0], label_rows, q, Q, plane_peer)
    send_rows(1, coarse, coarse_rows, zi, NZ, line_peer)

    start = masked(over_copies(receive_faces(0, started)))
    out_solution[...] = start.reshape(16, 16, 128)
    defect = source[...].reshape(FIELD) - apply_operator(start)
    held = masked(defect)
    flat_x = [held[a, i, 0] + held[a, i, 1] for a in range(2) for i in range(8)]
    sums_x = [
        functools.reduce(jnp.add, flat_x[:8] + [PHI_0[i] * flat_x[8 + i] for i in range(8)]),
        functools.reduce(jnp.add, [PHI_1[i] * flat_x[8 + i] for i in range(8)]),
    ]
    rhs_row = jnp.zeros((1, 128), jnp.float32)
    for a in range(2):
        along = jnp.sum(sums_x[a], axis=0, keepdims=True)
        for b in range(3):
            value = jnp.sum(along * block_z[b], axis=1, keepdims=True)
            rhs_row = jnp.where(lane1 == slot_base + (3 * a + b), value, rhs_row)
    row_send[1] = rhs_row
    send_rows(2, row_send.at[1], rhs_rows, q, Q, plane_peer)

    defect = add_inside(defect)
    send_faces(1, defect)

    wait_rows(0, label_rows)
    NR = coarse.shape[1] // 128
    rows_of = []
    used = (lane1 & 7) < 6
    for g in range(GROUPS):
        packed = jnp.sum(label_rows[pl.ds(g * GROUP, GROUP)], axis=0).astype(jnp.int32)
        packed = jnp.where(used, packed, -1)
        onehot[g] = jnp.where(iota((128, 128), 0) == (packed & 127), 1.0, 0.0)
        rows_of.append(packed >> 7)

    wait_rows(2, rhs_rows)
    rhs = jnp.zeros((16, 128), jnp.float32)
    for g in range(GROUPS):
        packed = jnp.sum(rhs_rows[pl.ds(g * GROUP, GROUP)], axis=0)
        placed = jnp.where(iota((16, 128), 0) == rows_of[g], packed, 0.0)
        rhs = rhs + lax.dot_general(
            placed,
            onehot[g],
            (((1,), (1,)), ((), ())),
            precision=HIGHEST,
            preferred_element_type=jnp.float32,
        )
    wait_rows(1, coarse_rows)
    partial = jnp.zeros((NZ, 2, 128), jnp.float32)
    for r in range(NR):
        partial = partial + coarse_rows[:, :, r * 128 : (r + 1) * 128] * rhs[r : r + 1][None]
    partial = jnp.sum(partial, axis=2, keepdims=True)
    PACK = 128 // (2 * NZ)
    PACK = min(PACK, Q)
    lane_of = (
        lax.rem(q, PACK) * (2 * NZ) + 2 * iota((NZ, 2, 128), 0) + iota((NZ, 2, 128), 1)
    )
    partial = jnp.where(iota((NZ, 2, 128), 2) == lane_of, partial, 0.0)
    row_send[2] = jnp.sum(jnp.sum(partial, axis=0), axis=0, keepdims=True)
    send_rows(3, row_send.at[2], line_rows, zi, NZ, line_peer)

    residual = masked(receive_faces(1, defect))
    out_residual[...] = residual.reshape(16, 16, 128)
    solved = add_inside(local_solve(residual))
    send_faces(2, solved)

    wait_rows(3, line_rows)
    row_send[3] = jnp.sum(line_rows[...], axis=0)
    send_rows(4, row_send.at[3], value_rows, q, Q, plane_peer)

    local = receive_faces(2, solved)

    wait_rows(4, value_rows)
    value_groups = [jnp.sum(value_rows[pl.ds(g * PACK, PACK)], axis=0) for g in range(Q // PACK)]
    coarse_values = []
    for s in range(6):
        number = jnp.full((1, 128), own_labels[s], jnp.int32)
        bit = number & 1
        device = number >> 1
        label_x, label_z = device // GZ, device % GZ
        row = (label_x // ZL) * YC + label_z % YC
        line = (label_z // YC) * ZL + label_x % ZL
        lane = (row % PACK) * (2 * NZ) + 2 * line + bit
        picked = jnp.zeros((1, 128), jnp.float32)
        for g in range(Q // PACK):
            picked = picked + jnp.where((lane1 == lane) & (row // PACK == g), value_groups[g], 0.0)
        coarse_values.append(jnp.sum(picked, axis=1, keepdims=True))
    first = functools.reduce(jnp.add, [coarse_values[b] * block_z[b] for b in range(3)])
    second = functools.reduce(jnp.add, [coarse_values[3 + b] * block_z[b] for b in range(3)])
    shapes = [[first] * 8, [PHI_0[i] * first + PHI_1[i] * second for i in range(8)]]
    precond = masked(
        join([[[local[a, i, b] + shapes[a][i] for b in range(2)] for i in range(8)] for a in range(2)])
    )
    applied = apply_operator(precond)
    residual = out_residual[...].reshape(FIELD)
    numerator = total(over_copies(residual * precond))
    denominator = total(precond * applied)
    row_send[4] = jnp.where(lane1 == 0, numerator, jnp.where(lane1 == 1, denominator, 0.0))
    send_rows(5, row_send.at[4], sum_rows, q, Q, plane_peer)

    image = add_inside(applied)
    send_faces(3, image)
    wait_rows(5, sum_rows)
    row_send[5] = jnp.sum(sum_rows[...], axis=0)
    send_rows(6, row_send.at[5], total_rows, zi, NZ, line_peer)
    image = masked(receive_faces(3, image))
    wait_rows(6, total_rows)
    totals = jnp.sum(total_rows[...], axis=0)
    numerator = jnp.sum(jnp.where(lane1 == 0, totals, 0.0), axis=1, keepdims=True)
    denominator = jnp.sum(jnp.where(lane1 == 1, totals, 0.0), axis=1, keepdims=True)
    alpha = numerator / denominator
    out_solution[...] = out_solution[...] + alpha[None] * precond.reshape(16, 16, 128)
    out_residual[...] = out_residual[...] - alpha[None] * image.reshape(16, 16, 128)

    for n in range(4):
        for s in range(2):
            pltpu.make_async_copy(x_send.at[n, s], x_send.at[n, s], x_sent.at[n, s]).wait()
        for s in range(6):
            pltpu.make_async_copy(z_send.at[n, s], z_send.at[n, s], z_sent.at[n, s]).wait()
    wait_sent(0, label_rows, Q)
    wait_sent(1, coarse_rows, NZ)
    wait_sent(2, rhs_rows, Q)
    wait_sent(3, line_rows, NZ)
    wait_sent(4, value_rows, Q)
    wait_sent(5, sum_rows, Q)
    wait_sent(6, total_rows, NZ)


def split_axes(mesh):
    runs, far = 4, max(2, mesh.shape["gz"] // 16)
    return mesh.shape["gx"] // runs, runs, far, mesh.shape["gz"] // far


def solution(mesh):
    shape = split_axes(mesh)
    XS, ZL, ZH, YC = shape
    Q, NZ = XS * YC, ZL * ZH

    def body(source, previous, coefficients, stiffness, vectors, eigen, coarse, labels):
        vmem = pl.BlockSpec(memory_space=pltpu.VMEM)
        smem = pl.BlockSpec(memory_space=pltpu.SMEM)
        f32 = jnp.float32
        return pl.pallas_call(
            functools.partial(tile_kernel, shape),
            out_shape=(
                jax.ShapeDtypeStruct(source.shape, f32),
                jax.ShapeDtypeStruct(source.shape, f32),
            ),
            in_specs=[vmem, vmem, vmem, smem, smem, smem, vmem, smem],
            out_specs=(vmem, vmem),
            scratch_shapes=[
                pltpu.VMEM((4, 2, 16, 128), f32),
                pltpu.VMEM((4, 2, 16, 128), f32),
                pltpu.VMEM((4, 6, 1, 256), f32),
                pltpu.VMEM((4, 6, 1, 256), f32),
                pltpu.VMEM((6, 1, 128), f32),
                pltpu.VMEM((Q, 1, 128), f32),
                pltpu.VMEM((Q, 1, 128), f32),
                pltpu.VMEM((NZ, 1, 128), f32),
                pltpu.VMEM((Q, 1, 128), f32),
                pltpu.VMEM((Q, 1, 128), f32),
                pltpu.VMEM((NZ, 1, 128), f32),
                pltpu.VMEM((NZ, 2, coarse.shape[1]), f32),
                pltpu.VMEM((max(1, Q // 16), 128, 128), f32),
                pltpu.SemaphoreType.DMA((4, 2)),
                pltpu.SemaphoreType.DMA((4, 6)),
                pltpu.SemaphoreType.DMA((4, 2)),
                pltpu.SemaphoreType.DMA((4, 6)),
                pltpu.SemaphoreType.DMA((7,)),
                pltpu.SemaphoreType.DMA((7,)),
            ],
            compiler_params=pltpu.CompilerParams(collective_id=0, has_side_effects=True),
        )(source, previous, coefficients, stiffness, vectors, eigen, coarse, labels)

    placed = (
        P("gx", None, "gz"),
        P("gx", None, "gz"),
        P(None, "gx", None, "gz"),
        P(),
        P(),
        P(),
        P(("gx", "gz"), None),
        P(None, "gx", None, "gz"),
    )
    return jax.shard_map(
        body,
        mesh=mesh,
        in_specs=placed,
        out_specs=(P("gx", None, "gz"), P("gx", None, "gz")),
        check_vma=False,
    )
```

```python
import functools

import jax
import jax.numpy as jnp
from jax import lax
from jax.experimental import pallas as pl
from jax.experimental.pallas import tpu as pltpu
from jax.sharding import PartitionSpec as P

MESH = pl.DeviceIdType.MESH
HIGHEST = lax.Precision.HIGHEST

GLL_POINTS = [
    -1.0,
    -0.8717401485096066,
    -0.5917001814331423,
    -0.2092992179024789,
    0.2092992179024789,
    0.5917001814331423,
    0.8717401485096066,
    1.0,
]
GLL_WEIGHTS = [
    0.03571428571428571,
    0.21070422714350603,
    0.34112269248350435,
    0.4124587946587038,
    0.4124587946587038,
    0.34112269248350435,
    0.21070422714350603,
    0.03571428571428571,
]
PHI_0 = [(1.0 - s) / 2.0 for s in GLL_POINTS]
PHI_1 = [(1.0 + s) / 2.0 for s in GLL_POINTS]

FIELD = (2, 8, 2, 8, 128)
ROWS = (256, 128)


def iota(shape, dim):
    return lax.broadcasted_iota(jnp.int32, shape, dim)


def table(index, values):
    result = jnp.full(index.shape, values[0], jnp.float32)
    for i in range(1, len(values)):
        result = jnp.where(index == i, values[i], result)
    return result


def tile_kernel(
    shape,
    source_in,
    previous_in,
    coefficients_in,
    stiffness_in,
    vectors_in,
    eigen_in,
    coarse_in,
    labels_in,
    start_out,
    precond_out,
    residual_out,
    image_out,
    alpha_out,
    source,
    previous,
    coefficients,
    stiffness,
    vectors,
    eigen,
    labels,
    x_send,
    x_recv,
    z_send,
    z_recv,
    row_send,
    label_rows,
    rhs_rows,
    line_rows,
    value_rows,
    sum_rows,
    total_rows,
    coarse_rows,
    onehot,
    x_sems,
    z_sems,
    x_sent,
    z_sent,
    row_sems,
    row_sent,
    far_sems,
    far_sent,
    near_sems,
    in_sems,
):
    XS, ZL, ZH, YC = shape
    Q, NZ = XS * YC, ZL * ZH
    gx, gz = lax.axis_index("gx"), lax.axis_index("gz")
    x, zl = lax.div(gx, ZL), lax.rem(gx, ZL)
    zh, yc = lax.div(gz, YC), lax.rem(gz, YC)
    q, zi = x * YC + yc, zh * ZL + zl
    parity, half = lax.rem(zi, 2), lax.div(zi, 2)
    GX, GZ = XS * ZL, ZH * YC
    left, right = lax.rem(gx + GX - 1, GX), lax.rem(gx + 1, GX)
    down, up = lax.rem(gz + GZ - 1, GZ), lax.rem(gz + 1, GZ)

    def plane_peer(k):
        other = lax.rem(q + k, Q)
        return {"gx": lax.div(other, YC) * ZL + zl, "gz": zh * YC + lax.rem(other, YC)}

    def line_peer(k):
        other = lax.rem(zi + k, NZ)
        return {"gx": x * ZL + lax.rem(other, ZL), "gz": lax.div(other, ZL) * YC + yc}

    neighbours = [
        (left, gz),
        (right, gz),
        (gx, down),
        (gx, up),
        (left, down),
        (left, up),
        (right, down),
        (right, up),
    ]

    barrier = pltpu.get_barrier_semaphore()
    for a, b in neighbours:
        pl.semaphore_signal(barrier, inc=1, device_id={"gx": a, "gz": b}, device_id_type=MESH)

    def greet_line(k, carry):
        pl.semaphore_signal(barrier, inc=1, device_id=line_peer(k), device_id_type=MESH)
        return carry

    def greet_plane(k, carry):
        pl.semaphore_signal(barrier, inc=1, device_id=plane_peer(k), device_id_type=MESH)
        return carry

    lax.fori_loop(1, NZ, greet_line, 0, unroll=5 if NZ == 16 else 1)
    lax.fori_loop(1, Q, greet_plane, 0, unroll=7 if Q == 64 else 1)

    fetches = [
        pltpu.make_async_copy(a, b, in_sems.at[i])
        for i, (a, b) in enumerate(
            [
                (previous_in, previous),
                (labels_in, labels),
                (coarse_in, coarse_rows.at[parity, half]),
                (coefficients_in, coefficients),
                (stiffness_in, stiffness),
                (vectors_in, vectors),
                (eigen_in, eigen),
                (source_in, source),
            ]
        )
    ]
    for fetch in fetches:
        fetch.start()

    lane8 = iota((8, 128), 1)
    sub8 = iota((8, 128), 0)
    lane1 = iota((1, 128), 1)
    inner = lane8 & 7
    inner1 = lane1 & 7
    element1 = lane1 >> 3
    weight_z = table(inner, GLL_WEIGHTS)
    weight_y = table(sub8, GLL_WEIGHTS)
    edge_z = (inner == 0) | (inner == 7)
    half_z = jnp.where(edge_z, 0.5, 1.0)
    inv_yz = [jnp.where(sub8 == 7, 0.5, 1.0) * half_z, jnp.where(sub8 == 0, 0.5, 1.0) * half_z]
    keep_y = jnp.where(sub8 == 7, 0.0, 1.0)
    inv_x = [0.5, 1.0, 1.0, 1.0, 1.0, 1.0, 1.0, 0.5]

    def join(parts):
        return jnp.stack(
            [jnp.stack([jnp.stack(parts[a][i]) for i in range(8)]) for a in range(2)]
        )

    for fetch in fetches:
        fetch.wait()

    spread_matrix = ((iota((16, 128), 1) >> 3) == iota((16, 128), 0)).astype(jnp.float32)
    spreads = []
    for c in range(3):
        per_x = []
        for a in range(2):
            rows = jnp.dot(
                coefficients[c, a], spread_matrix, precision=HIGHEST, preferred_element_type=jnp.float32
            )
            per_x.append([jnp.broadcast_to(rows[b : b + 1], (8, 128)) for b in range(2)])
        spreads.append(per_x)

    def columns(matrix, transposed):
        return [
            table(sub8, [matrix[p, j] if transposed else matrix[j, p] for j in range(8)]) for p in range(8)
        ]

    def block_matrix(matrix_columns):
        tile = matrix_columns[0]
        for p in range(1, 8):
            tile = jnp.where(inner == p, matrix_columns[p], tile)
        full = jnp.concatenate([tile] * 16, axis=0)
        same = (iota((128, 128), 0) >> 3) == (iota((128, 128), 1) >> 3)
        return jnp.where(same, full, 0.0)

    stiff_columns = columns(stiffness, False)
    vector_columns = columns(vectors, False)
    vector_rows = columns(vectors, True)
    stiff_z = block_matrix(columns(stiffness, True))
    forward_z = block_matrix(vector_columns)
    backward_z = block_matrix(vector_rows)

    def along_x(v, entry):
        return jnp.stack(
            [
                jnp.stack([functools.reduce(jnp.add, [entry(i, p) * v[a, p] for p in range(8)]) for i in range(8)])
                for a in range(2)
            ]
        )

    def along_y(v, cols):
        return functools.reduce(
            jnp.add, [cols[p] * jnp.broadcast_to(v[:, :, :, p : p + 1, :], FIELD) for p in range(8)]
        )

    def along_z(v, matrix):
        return jnp.dot(
            v.reshape(ROWS), matrix, precision=HIGHEST, preferred_element_type=jnp.float32
        ).reshape(FIELD)

    factor_x = [[spreads[0][a][b] * weight_y * weight_z for b in range(2)] for a in range(2)]
    factor_y = [[spreads[1][a][b] * weight_z for b in range(2)] for a in range(2)]
    factor_z = [[spreads[2][a][b] * weight_y for b in range(2)] for a in range(2)]

    def apply_operator(v):
        vx = along_x(v, lambda i, p: stiffness[i, p])
        vy = along_y(v, stiff_columns)
        vz = along_z(v, stiff_z)
        return join(
            [
                [
                    [
                        factor_x[a][b] * vx[a, i, b]
                        + GLL_WEIGHTS[i] * (factor_y[a][b] * vy[a, i, b] + factor_z[a][b] * vz[a, i, b])
                        for b in range(2)
                    ]
                    for i in range(8)
                ]
                for a in range(2)
            ]
        )

    def local_solve(v):
        t = along_x(v, lambda i, p: vectors[p, i])
        t = along_y(t, vector_rows)
        t = along_z(t, forward_z)
        lam_y = table(sub8, [eigen[k] for k in range(8)])
        lam_z = table(inner, [eigen[k] for k in range(8)])
        rest = [[spreads[1][a][b] * lam_y + spreads[2][a][b] * lam_z for b in range(2)] for a in range(2)]
        t = join(
            [
                [[t[a, i, b] / (spreads[0][a][b] * eigen[i] + rest[a][b]) for b in range(2)] for i in range(8)]
                for a in range(2)
            ]
        )
        t = along_x(t, lambda i, p: vectors[i, p])
        t = along_y(t, vector_columns)
        return along_z(t, backward_z)

    low_z = (inner == 0) & (lane8 > 0)
    high_z = (inner == 7) & (lane8 < 127)

    def add_inside(v):
        flat = v.reshape(ROWS)
        after = pltpu.roll(flat, 127, 1).reshape(FIELD)
        before = pltpu.roll(flat, 1, 1).reshape(FIELD)
        v = v + jnp.where(high_z, after, 0.0) + jnp.where(low_z, before, 0.0)
        first, second = v[:, :, 0], v[:, :, 1]
        to_first = jnp.broadcast_to(second[:, :, 0:1, :], (2, 8, 8, 128))
        to_second = jnp.broadcast_to(first[:, :, 7:8, :], (2, 8, 8, 128))
        first = first + jnp.where(sub8 == 7, to_first, 0.0)
        second = second + jnp.where(sub8 == 0, to_second, 0.0)
        v = jnp.stack([first, second], axis=2)
        seam = v[0, 7] + v[1, 0]
        return jnp.stack(
            [
                jnp.concatenate([v[0, :7], seam[None]], axis=0),
                jnp.concatenate([seam[None], v[1, 1:]], axis=0),
            ]
        )

    picker = jnp.where(((sub8 == 0) & (lane8 == 0)) | ((sub8 == 1) & (lane8 == 127)), 1.0, 0.0)
    wide = iota((8, 256), 1)

    def send_faces(n, v):
        x_send[n, 0] = v[0, 0].reshape(16, 128)
        x_send[n, 1] = v[1, 7].reshape(16, 128)
        faces = lax.dot_general(
            picker,
            v.reshape(ROWS),
            (((1,), (1,)), ((), ())),
            precision=HIGHEST,
            preferred_element_type=jnp.float32,
        )
        plus = jnp.where(wide < 16, pltpu.roll(faces, 16, 1), 0.0)
        minus = jnp.where(wide >= 240, pltpu.roll(faces, 240, 1), 0.0)
        for k, value in enumerate((faces, plus, minus)):
            z_send[n, 2 * k] = value[0:1]
            z_send[n, 2 * k + 1] = value[1:2]
        plan = [
            (0, 3, gx, down),
            (1, 0, gx, up),
            (2, 4, right, down),
            (3, 1, right, up),
            (4, 5, left, down),
            (5, 2, left, up),
        ]
        for src, dst, a, b in plan:
            pltpu.make_async_remote_copy(
                src_ref=z_send.at[n, src],
                dst_ref=z_recv.at[n, dst],
                send_sem=z_sent.at[n, src],
                recv_sem=z_sems.at[n, dst],
                device_id={"gx": a, "gz": b},
                device_id_type=MESH,
            ).start()
        for src, dst, a in ((0, 1, left), (1, 0, right)):
            pltpu.make_async_remote_copy(
                src_ref=x_send.at[n, src],
                dst_ref=x_recv.at[n, dst],
                send_sem=x_sent.at[n, src],
                recv_sem=x_sems.at[n, dst],
                device_id={"gx": a, "gz": gz},
                device_id_type=MESH,
            ).start()

    def receive_faces(n, v):
        for s in range(2):
            pltpu.make_async_copy(x_recv.at[n, s], x_recv.at[n, s], x_sems.at[n, s]).wait()
        for s in range(6):
            pltpu.make_async_copy(z_recv.at[n, s], z_recv.at[n, s], z_sems.at[n, s]).wait()
        low = z_recv[n, 0] + z_recv[n, 1] + z_recv[n, 2]
        high = z_recv[n, 3] + z_recv[n, 4] + z_recv[n, 5]
        sub = iota((8, 256), 0)
        both = jnp.where(sub == 0, jnp.broadcast_to(low, (8, 256)), 0.0)
        both = jnp.where(sub == 1, jnp.broadcast_to(high, (8, 256)), both)
        add = lax.dot_general(
            both, picker, (((0,), (0,)), ((), ())), precision=HIGHEST, preferred_element_type=jnp.float32
        ).reshape(FIELD)
        v = v + add
        top = v[0, 0] + x_recv[n, 0].reshape(2, 8, 128)
        bottom = v[1, 7] + x_recv[n, 1].reshape(2, 8, 128)
        return jnp.stack(
            [
                jnp.concatenate([top[None], v[0, 1:]], axis=0),
                jnp.concatenate([v[1, :7], bottom[None]], axis=0),
            ]
        )

    def masked(v):
        return jnp.stack([v[:, :, 0], v[:, :, 1] * keep_y], axis=2)

    def over_copies(v):
        return join(
            [[[v[a, i, b] * (inv_yz[b] * inv_x[i]) for b in range(2)] for i in range(8)] for a in range(2)]
        )

    def total(v):
        rows = jnp.sum(v.reshape(32, 8, 128), axis=0)
        return jnp.sum(jnp.sum(rows, axis=1, keepdims=True), axis=0, keepdims=True)

    def send_rows(n, src, rows, slot, count, peer):
        pltpu.make_async_copy(src, rows.at[slot], row_sems.at[n]).start()

        def step(k, carry):
            pltpu.make_async_remote_copy(
                src_ref=src,
                dst_ref=rows.at[slot],
                send_sem=row_sent.at[n],
                recv_sem=row_sems.at[n],
                device_id=peer(k),
                device_id_type=MESH,
            ).start()
            return carry

        lax.fori_loop(1, count, step, 0, unroll={64: 7, 16: 5}.get(count, 1))

    def wait_rows(n, rows):
        pltpu.make_async_copy(rows, rows, row_sems.at[n]).wait()

    def wait_sent(n, rows, count):
        part = rows.at[pl.ds(0, count - 1)]
        pltpu.make_async_copy(part, part, row_sent.at[n]).wait()

    ramp_0, ramp_1 = table(inner1, PHI_0), table(inner1, PHI_1)
    one, zero = jnp.ones((1, 128), jnp.float32), jnp.zeros((1, 128), jnp.float32)
    block_z = [
        jnp.where(element1 < 7, one, jnp.where(element1 == 7, ramp_0, zero)),
        jnp.where(
            element1 == 7,
            ramp_1,
            jnp.where(element1 == 15, ramp_0, jnp.where(element1 > 7, one, zero)),
        ),
        jnp.where(element1 == 15, ramp_1, zero),
    ]
    own_labels = [
        labels[0, 0, 0, 0],
        labels[0, 0, 0, 8],
        labels[1, 0, 0, 15],
        labels[4, 1, 0, 0],
        labels[4, 1, 0, 8],
        labels[5, 1, 0, 15],
    ]
    GROUP = min(16, Q)
    GROUPS = Q // GROUP
    slot_base = 8 * lax.rem(q, GROUP)

    label_row = jnp.zeros((1, 128), jnp.float32)
    for s in range(6):
        label_row = jnp.where(lane1 == slot_base + s, own_labels[s].astype(jnp.float32), label_row)
    row_send[0] = label_row

    started = add_inside(previous[...].reshape(FIELD))

    pl.semaphore_wait(barrier, 8 + (NZ - 1) + (Q - 1))

    send_faces(0, started)
    send_rows(0, row_send.at[0], label_rows, q, Q, plane_peer)

    def far(k, carry):
        pltpu.make_async_remote_copy(
            src_ref=coarse_rows.at[parity, half],
            dst_ref=coarse_rows.at[parity, half],
            send_sem=far_sent,
            recv_sem=far_sems,
            device_id=line_peer(2 * k),
            device_id_type=MESH,
        ).start()
        return carry

    lax.fori_loop(1, NZ // 2, far, 0, unroll=7 if NZ == 16 else 1)

    start = masked(over_copies(receive_faces(0, started)))
    start_out[...] = start.reshape(16, 16, 128)
    defect = source[...].reshape(FIELD) - apply_operator(start)
    held = masked(defect)
    flat_x = [held[a, i, 0] + held[a, i, 1] for a in range(2) for i in range(8)]
    sums_x = [
        functools.reduce(jnp.add, flat_x[:8] + [PHI_0[i] * flat_x[8 + i] for i in range(8)]),
        functools.reduce(jnp.add, [PHI_1[i] * flat_x[8 + i] for i in range(8)]),
    ]
    rhs_row = jnp.zeros((1, 128), jnp.float32)
    for a in range(2):
        along = jnp.sum(sums_x[a], axis=0, keepdims=True)
        for b in range(3):
            value = jnp.sum(along * block_z[b], axis=1, keepdims=True)
            rhs_row = jnp.where(lane1 == slot_base + (3 * a + b), value, rhs_row)
    row_send[1] = rhs_row
    send_rows(2, row_send.at[1], rhs_rows, q, Q, plane_peer)

    others = coarse_rows.at[parity, pl.ds(0, NZ // 2 - 1)]
    pltpu.make_async_copy(others, others, far_sems).wait()
    beside = pltpu.make_async_remote_copy(
        src_ref=coarse_rows.at[parity],
        dst_ref=coarse_rows.at[parity],
        send_sem=near_sems.at[0],
        recv_sem=near_sems.at[1],
        device_id=line_peer(NZ + 1 - 2 * parity),
        device_id_type=MESH,
    )
    beside.start()

    defect = add_inside(defect)
    send_faces(1, defect)

    wait_rows(0, label_rows)
    NR = coarse_in.shape[1] // 128
    rows_of = []
    used = (lane1 & 7) < 6
    for g in range(GROUPS):
        packed = jnp.sum(label_rows[pl.ds(g * GROUP, GROUP)], axis=0).astype(jnp.int32)
        packed = jnp.where(used, packed, -1)
        onehot[g] = jnp.where(iota((128, 128), 0) == (packed & 127), 1.0, 0.0)
        rows_of.append(packed >> 7)

    wait_rows(2, rhs_rows)
    rhs = jnp.zeros((16, 128), jnp.float32)
    for g in range(GROUPS):
        packed = jnp.sum(rhs_rows[pl.ds(g * GROUP, GROUP)], axis=0)
        placed = jnp.where(iota((16, 128), 0) == rows_of[g], packed, 0.0)
        rhs = rhs + lax.dot_general(
            placed,
            onehot[g],
            (((1,), (1,)), ((), ())),
            precision=HIGHEST,
            preferred_element_type=jnp.float32,
        )
    beside.wait_recv()
    PACK = min(128 // (2 * NZ), Q)
    wide_rows = (NZ // 2, 2, 128)
    line_sum = jnp.zeros((2, 128), jnp.float32)
    for half_line in range(2):
        partial = jnp.zeros(wide_rows, jnp.float32)
        for r in range(NR):
            partial = partial + coarse_rows[half_line, :, :, r * 128 : (r + 1) * 128] * rhs[r : r + 1][None]
        partial = jnp.sum(partial, axis=2, keepdims=True)
        member = 2 * iota(wide_rows, 0) + half_line
        lane_of = lax.rem(q, PACK) * (2 * NZ) + 2 * member + iota(wide_rows, 1)
        line_sum = line_sum + jnp.sum(jnp.where(iota(wide_rows, 2) == lane_of, partial, 0.0), axis=0)
    row_send[2] = jnp.sum(line_sum, axis=0, keepdims=True)
    send_rows(3, row_send.at[2], line_rows, zi, NZ, line_peer)

    residual = masked(receive_faces(1, defect))
    residual_out[...] = residual.reshape(16, 16, 128)
    solved = add_inside(local_solve(residual))
    send_faces(2, solved)

    wait_rows(3, line_rows)
    row_send[3] = jnp.sum(line_rows[...], axis=0)
    send_rows(4, row_send.at[3], value_rows, q, Q, plane_peer)

    local = receive_faces(2, solved)

    wait_rows(4, value_rows)
    value_groups = [jnp.sum(value_rows[pl.ds(g * PACK, PACK)], axis=0) for g in range(Q // PACK)]
    coarse_values = []
    for s in range(6):
        number = jnp.full((1, 128), own_labels[s], jnp.int32)
        bit = number & 1
        device = number >> 1
        label_x, label_z = device // GZ, device % GZ
        row = (label_x // ZL) * YC + label_z % YC
        line = (label_z // YC) * ZL + label_x % ZL
        lane = (row % PACK) * (2 * NZ) + 2 * line + bit
        picked = jnp.zeros((1, 128), jnp.float32)
        for g in range(Q // PACK):
            picked = picked + jnp.where((lane1 == lane) & (row // PACK == g), value_groups[g], 0.0)
        coarse_values.append(jnp.sum(picked, axis=1, keepdims=True))
    first = functools.reduce(jnp.add, [coarse_values[b] * block_z[b] for b in range(3)])
    second = functools.reduce(jnp.add, [coarse_values[3 + b] * block_z[b] for b in range(3)])
    shapes = [[first] * 8, [PHI_0[i] * first + PHI_1[i] * second for i in range(8)]]
    precond = masked(
        join([[[local[a, i, b] + shapes[a][i] for b in range(2)] for i in range(8)] for a in range(2)])
    )
    applied = apply_operator(precond)
    residual = residual_out[...].reshape(FIELD)
    numerator = total(over_copies(residual * precond))
    denominator = total(precond * applied)
    row_send[4] = jnp.where(lane1 == 0, numerator, jnp.where(lane1 == 1, denominator, 0.0))
    send_rows(5, row_send.at[4], sum_rows, q, Q, plane_peer)

    image = add_inside(applied)
    send_faces(3, image)
    wait_rows(5, sum_rows)
    row_send[5] = jnp.sum(sum_rows[...], axis=0)
    send_rows(6, row_send.at[5], total_rows, zi, NZ, line_peer)
    precond_out[...] = precond.reshape(16, 16, 128)
    image_out[...] = masked(receive_faces(3, image)).reshape(16, 16, 128)
    wait_rows(6, total_rows)
    totals = jnp.sum(total_rows[...], axis=0)
    numerator = jnp.sum(jnp.where(lane1 == 0, totals, 0.0), axis=1, keepdims=True)
    denominator = jnp.sum(jnp.where(lane1 == 1, totals, 0.0), axis=1, keepdims=True)
    alpha_out[...] = jnp.broadcast_to(numerator / denominator, (1, 128))

    for n in range(4):
        for s in range(2):
            pltpu.make_async_copy(x_send.at[n, s], x_send.at[n, s], x_sent.at[n, s]).wait()
        for s in range(6):
            pltpu.make_async_copy(z_send.at[n, s], z_send.at[n, s], z_sent.at[n, s]).wait()
    wait_sent(0, label_rows, Q)
    pltpu.make_async_copy(others, others, far_sent).wait()
    beside.wait_send()
    wait_sent(2, rhs_rows, Q)
    wait_sent(3, line_rows, NZ)
    wait_sent(4, value_rows, Q)
    wait_sent(5, sum_rows, Q)
    wait_sent(6, total_rows, NZ)


def split_axes(mesh):
    runs, far = 4, max(2, mesh.shape["gz"] // 16)
    return mesh.shape["gx"] // runs, runs, far, mesh.shape["gz"] // far


def solution(mesh):
    shape = split_axes(mesh)
    XS, ZL, ZH, YC = shape
    Q, NZ = XS * YC, ZL * ZH

    def body(source, previous, coefficients, stiffness, vectors, eigen, coarse, labels):
        f32 = jnp.float32
        field = pltpu.VMEM(source.shape, f32)
        operands = (source, previous, coefficients, stiffness, vectors, eigen, coarse, labels)
        start, precond, residual, image, alpha = pl.pallas_call(
            functools.partial(tile_kernel, shape),
            out_shape=(field, field, field, field, pltpu.VMEM((1, 128), f32)),
            in_specs=[pl.BlockSpec(memory_space=pl.ANY)] * 8,
            out_specs=(pl.BlockSpec(memory_space=pltpu.VMEM),) * 5,
            scratch_shapes=[
                pltpu.VMEM(source.shape, f32),
                pltpu.VMEM(source.shape, f32),
                pltpu.VMEM(coefficients.shape, f32),
                pltpu.SMEM(stiffness.shape, f32),
                pltpu.SMEM(vectors.shape, f32),
                pltpu.SMEM(eigen.shape, f32),
                pltpu.SMEM(labels.shape, jnp.int32),
                pltpu.VMEM((4, 2, 16, 128), f32),
                pltpu.VMEM((4, 2, 16, 128), f32),
                pltpu.VMEM((4, 6, 1, 256), f32),
                pltpu.VMEM((4, 6, 1, 256), f32),
                pltpu.VMEM((6, 1, 128), f32),
                pltpu.VMEM((Q, 1, 128), f32),
                pltpu.VMEM((Q, 1, 128), f32),
                pltpu.VMEM((NZ, 1, 128), f32),
                pltpu.VMEM((Q, 1, 128), f32),
                pltpu.VMEM((Q, 1, 128), f32),
                pltpu.VMEM((NZ, 1, 128), f32),
                pltpu.VMEM((2, NZ // 2, 2, coarse.shape[1]), f32),
                pltpu.VMEM((max(1, Q // 16), 128, 128), f32),
                pltpu.SemaphoreType.DMA((4, 2)),
                pltpu.SemaphoreType.DMA((4, 6)),
                pltpu.SemaphoreType.DMA((4, 2)),
                pltpu.SemaphoreType.DMA((4, 6)),
                pltpu.SemaphoreType.DMA((7,)),
                pltpu.SemaphoreType.DMA((7,)),
                pltpu.SemaphoreType.DMA,
                pltpu.SemaphoreType.DMA,
                pltpu.SemaphoreType.DMA((2,)),
                pltpu.SemaphoreType.DMA((8,)),
            ],
            compiler_params=pltpu.CompilerParams(collective_id=0, has_side_effects=True),
        )(*operands)
        alpha = alpha[None]
        return start + alpha * precond, residual - alpha * image

    placed = (
        P("gx", None, "gz"),
        P("gx", None, "gz"),
        P(None, "gx", None, "gz"),
        P(),
        P(),
        P(),
        P(("gx", "gz"), None),
        P(None, "gx", None, "gz"),
    )
    return jax.shard_map(
        body,
        mesh=mesh,
        in_specs=placed,
        out_specs=(P("gx", None, "gz"), P("gx", None, "gz")),
        check_vma=False,
    )
```

```python
import functools

import jax
import jax.numpy as jnp
from jax import lax
from jax.experimental import pallas as pl
from jax.experimental.pallas import tpu as pltpu
from jax.sharding import PartitionSpec as P

MESH = pl.DeviceIdType.MESH
HIGHEST = lax.Precision.HIGHEST

GLL_POINTS = [
    -1.0,
    -0.8717401485096066,
    -0.5917001814331423,
    -0.2092992179024789,
    0.2092992179024789,
    0.5917001814331423,
    0.8717401485096066,
    1.0,
]
GLL_WEIGHTS = [
    0.03571428571428571,
    0.21070422714350603,
    0.34112269248350435,
    0.4124587946587038,
    0.4124587946587038,
    0.34112269248350435,
    0.21070422714350603,
    0.03571428571428571,
]
PHI_0 = [(1.0 - s) / 2.0 for s in GLL_POINTS]
PHI_1 = [(1.0 + s) / 2.0 for s in GLL_POINTS]

FIELD = (2, 8, 2, 8, 128)
ROWS = (256, 128)


def iota(shape, dim):
    return lax.broadcasted_iota(jnp.int32, shape, dim)


def table(index, values):
    result = jnp.full(index.shape, values[0], jnp.float32)
    for i in range(1, len(values)):
        result = jnp.where(index == i, values[i], result)
    return result


def tile_kernel(
    shape,
    source_in,
    previous_in,
    coefficients_in,
    stiffness_in,
    vectors_in,
    eigen_in,
    coarse_in,
    labels_in,
    start_out,
    precond_out,
    residual_out,
    image_out,
    alpha_out,
    source,
    previous,
    coefficients,
    stiffness,
    vectors,
    eigen,
    labels,
    x_send,
    x_recv,
    z_send,
    z_recv,
    row_send,
    label_rows,
    rhs_rows,
    line_rows,
    value_rows,
    sum_rows,
    total_rows,
    coarse_rows,
    onehot,
    x_sems,
    z_sems,
    x_sent,
    z_sent,
    row_sems,
    row_sent,
    far_sems,
    far_sent,
    near_sems,
    in_sems,
):
    XS, ZL, ZH, YC = shape
    Q, NZ = XS * YC, ZL * ZH
    gx, gz = lax.axis_index("gx"), lax.axis_index("gz")
    x, zl = lax.div(gx, ZL), lax.rem(gx, ZL)
    zh, yc = lax.div(gz, YC), lax.rem(gz, YC)
    q, zi = x * YC + yc, zh * ZL + zl
    parity, half = lax.rem(zi, 2), lax.div(zi, 2)
    GX, GZ = XS * ZL, ZH * YC
    left, right = lax.rem(gx + GX - 1, GX), lax.rem(gx + 1, GX)
    down, up = lax.rem(gz + GZ - 1, GZ), lax.rem(gz + 1, GZ)

    def plane_peer(k):
        other = lax.rem(q + k, Q)
        return {"gx": lax.div(other, YC) * ZL + zl, "gz": zh * YC + lax.rem(other, YC)}

    def line_peer(k):
        other = lax.rem(zi + k, NZ)
        return {"gx": x * ZL + lax.rem(other, ZL), "gz": lax.div(other, ZL) * YC + yc}

    neighbours = [
        (left, gz),
        (right, gz),
        (gx, down),
        (gx, up),
        (left, down),
        (left, up),
        (right, down),
        (right, up),
    ]

    barrier = pltpu.get_barrier_semaphore()
    for a, b in neighbours:
        pl.semaphore_signal(barrier, inc=1, device_id={"gx": a, "gz": b}, device_id_type=MESH)

    def greet_line(k, carry):
        pl.semaphore_signal(barrier, inc=1, device_id=line_peer(k), device_id_type=MESH)
        return carry

    def greet_plane(k, carry):
        pl.semaphore_signal(barrier, inc=1, device_id=plane_peer(k), device_id_type=MESH)
        return carry

    lax.fori_loop(1, NZ, greet_line, 0, unroll=5 if NZ == 16 else 1)
    lax.fori_loop(1, Q, greet_plane, 0, unroll=7 if Q == 64 else 1)

    fetches = [
        pltpu.make_async_copy(a, b, in_sems.at[i])
        for i, (a, b) in enumerate(
            [
                (previous_in, previous),
                (labels_in, labels),
                (coarse_in, coarse_rows.at[parity, half]),
                (coefficients_in, coefficients),
                (stiffness_in, stiffness),
                (vectors_in, vectors),
                (eigen_in, eigen),
                (source_in, source),
            ]
        )
    ]
    for fetch in fetches:
        fetch.start()

    lane8 = iota((8, 128), 1)
    sub8 = iota((8, 128), 0)
    lane1 = iota((1, 128), 1)
    inner = lane8 & 7
    inner1 = lane1 & 7
    element1 = lane1 >> 3
    weight_z = table(inner, GLL_WEIGHTS)
    weight_y = table(sub8, GLL_WEIGHTS)
    edge_z = (inner == 0) | (inner == 7)
    half_z = jnp.where(edge_z, 0.5, 1.0)
    inv_yz = [jnp.where(sub8 == 7, 0.5, 1.0) * half_z, jnp.where(sub8 == 0, 0.5, 1.0) * half_z]
    keep_y = jnp.where(sub8 == 7, 0.0, 1.0)
    inv_x = [0.5, 1.0, 1.0, 1.0, 1.0, 1.0, 1.0, 0.5]

    def join(parts):
        return jnp.stack(
            [jnp.stack([jnp.stack(parts[a][i]) for i in range(8)]) for a in range(2)]
        )

    def columns(matrix, transposed):
        return [
            table(sub8, [matrix[p, j] if transposed else matrix[j, p] for j in range(8)]) for p in range(8)
        ]

    def block_matrix(matrix_columns):
        tile = matrix_columns[0]
        for p in range(1, 8):
            tile = jnp.where(inner == p, matrix_columns[p], tile)
        full = jnp.concatenate([tile] * 16, axis=0)
        same = (iota((128, 128), 0) >> 3) == (iota((128, 128), 1) >> 3)
        return jnp.where(same, full, 0.0)

    def along_x(v, entry):
        return jnp.stack(
            [
                jnp.stack([functools.reduce(jnp.add, [entry(i, p) * v[a, p] for p in range(8)]) for i in range(8)])
                for a in range(2)
            ]
        )

    def along_y(v, cols):
        return functools.reduce(
            jnp.add, [cols[p] * jnp.broadcast_to(v[:, :, :, p : p + 1, :], FIELD) for p in range(8)]
        )

    def along_z(v, matrix):
        return jnp.dot(
            v.reshape(ROWS), matrix, precision=HIGHEST, preferred_element_type=jnp.float32
        ).reshape(FIELD)

    def apply_operator(v):
        vx = along_x(v, lambda i, p: stiffness[i, p])
        vy = along_y(v, stiff_columns)
        vz = along_z(v, stiff_z)
        return join(
            [
                [
                    [
                        factor_x[a][b] * vx[a, i, b]
                        + GLL_WEIGHTS[i] * (factor_y[a][b] * vy[a, i, b] + factor_z[a][b] * vz[a, i, b])
                        for b in range(2)
                    ]
                    for i in range(8)
                ]
                for a in range(2)
            ]
        )

    def local_solve(v):
        t = along_x(v, lambda i, p: vectors[p, i])
        t = along_y(t, vector_rows)
        t = along_z(t, forward_z)
        lam_y = table(sub8, [eigen[k] for k in range(8)])
        lam_z = table(inner, [eigen[k] for k in range(8)])
        rest = [[spreads[1][a][b] * lam_y + spreads[2][a][b] * lam_z for b in range(2)] for a in range(2)]
        t = join(
            [
                [[t[a, i, b] / (spreads[0][a][b] * eigen[i] + rest[a][b]) for b in range(2)] for i in range(8)]
                for a in range(2)
            ]
        )
        t = along_x(t, lambda i, p: vectors[i, p])
        t = along_y(t, vector_columns)
        return along_z(t, backward_z)

    low_z = (inner == 0) & (lane8 > 0)
    high_z = (inner == 7) & (lane8 < 127)

    def add_inside(v):
        flat = v.reshape(ROWS)
        after = pltpu.roll(flat, 127, 1).reshape(FIELD)
        before = pltpu.roll(flat, 1, 1).reshape(FIELD)
        v = v + jnp.where(high_z, after, 0.0) + jnp.where(low_z, before, 0.0)
        first, second = v[:, :, 0], v[:, :, 1]
        to_first = jnp.broadcast_to(second[:, :, 0:1, :], (2, 8, 8, 128))
        to_second = jnp.broadcast_to(first[:, :, 7:8, :], (2, 8, 8, 128))
        first = first + jnp.where(sub8 == 7, to_first, 0.0)
        second = second + jnp.where(sub8 == 0, to_second, 0.0)
        v = jnp.stack([first, second], axis=2)
        seam = v[0, 7] + v[1, 0]
        return jnp.stack(
            [
                jnp.concatenate([v[0, :7], seam[None]], axis=0),
                jnp.concatenate([seam[None], v[1, 1:]], axis=0),
            ]
        )

    picker = jnp.where(((sub8 == 0) & (lane8 == 0)) | ((sub8 == 1) & (lane8 == 127)), 1.0, 0.0)
    wide = iota((8, 256), 1)

    def send_faces(n, v):
        x_send[n, 0] = v[0, 0].reshape(16, 128)
        x_send[n, 1] = v[1, 7].reshape(16, 128)
        faces = lax.dot_general(
            picker,
            v.reshape(ROWS),
            (((1,), (1,)), ((), ())),
            precision=HIGHEST,
            preferred_element_type=jnp.float32,
        )
        plus = jnp.where(wide < 16, pltpu.roll(faces, 16, 1), 0.0)
        minus = jnp.where(wide >= 240, pltpu.roll(faces, 240, 1), 0.0)
        for k, value in enumerate((faces, plus, minus)):
            z_send[n, 2 * k] = value[0:1]
            z_send[n, 2 * k + 1] = value[1:2]
        plan = [
            (0, 3, gx, down),
            (1, 0, gx, up),
            (2, 4, right, down),
            (3, 1, right, up),
            (4, 5, left, down),
            (5, 2, left, up),
        ]
        for src, dst, a, b in plan:
            pltpu.make_async_remote_copy(
                src_ref=z_send.at[n, src],
                dst_ref=z_recv.at[n, dst],
                send_sem=z_sent.at[n, src],
                recv_sem=z_sems.at[n, dst],
                device_id={"gx": a, "gz": b},
                device_id_type=MESH,
            ).start()
        for src, dst, a in ((0, 1, left), (1, 0, right)):
            pltpu.make_async_remote_copy(
                src_ref=x_send.at[n, src],
                dst_ref=x_recv.at[n, dst],
                send_sem=x_sent.at[n, src],
                recv_sem=x_sems.at[n, dst],
                device_id={"gx": a, "gz": gz},
                device_id_type=MESH,
            ).start()

    def receive_faces(n, v):
        for s in range(2):
            pltpu.make_async_copy(x_recv.at[n, s], x_recv.at[n, s], x_sems.at[n, s]).wait()
        for s in range(6):
            pltpu.make_async_copy(z_recv.at[n, s], z_recv.at[n, s], z_sems.at[n, s]).wait()
        low = z_recv[n, 0] + z_recv[n, 1] + z_recv[n, 2]
        high = z_recv[n, 3] + z_recv[n, 4] + z_recv[n, 5]
        sub = iota((8, 256), 0)
        both = jnp.where(sub == 0, jnp.broadcast_to(low, (8, 256)), 0.0)
        both = jnp.where(sub == 1, jnp.broadcast_to(high, (8, 256)), both)
        add = lax.dot_general(
            both, picker, (((0,), (0,)), ((), ())), precision=HIGHEST, preferred_element_type=jnp.float32
        ).reshape(FIELD)
        v = v + add
        top = v[0, 0] + x_recv[n, 0].reshape(2, 8, 128)
        bottom = v[1, 7] + x_recv[n, 1].reshape(2, 8, 128)
        return jnp.stack(
            [
                jnp.concatenate([top[None], v[0, 1:]], axis=0),
                jnp.concatenate([v[1, :7], bottom[None]], axis=0),
            ]
        )

    def masked(v):
        return jnp.stack([v[:, :, 0], v[:, :, 1] * keep_y], axis=2)

    def over_copies(v):
        return join(
            [[[v[a, i, b] * (inv_yz[b] * inv_x[i]) for b in range(2)] for i in range(8)] for a in range(2)]
        )

    def total(v):
        rows = jnp.sum(v.reshape(32, 8, 128), axis=0)
        return jnp.sum(jnp.sum(rows, axis=1, keepdims=True), axis=0, keepdims=True)

    def send_rows(n, src, rows, slot, count, peer):
        pltpu.make_async_copy(src, rows.at[slot], row_sems.at[n]).start()

        def step(k, carry):
            pltpu.make_async_remote_copy(
                src_ref=src,
                dst_ref=rows.at[slot],
                send_sem=row_sent.at[n],
                recv_sem=row_sems.at[n],
                device_id=peer(k),
                device_id_type=MESH,
            ).start()
            return carry

        lax.fori_loop(1, count, step, 0, unroll={64: 7, 16: 5}.get(count, 1))

    def wait_rows(n, rows):
        pltpu.make_async_copy(rows, rows, row_sems.at[n]).wait()

    def wait_sent(n, rows, count):
        part = rows.at[pl.ds(0, count - 1)]
        pltpu.make_async_copy(part, part, row_sent.at[n]).wait()

    ramp_0, ramp_1 = table(inner1, PHI_0), table(inner1, PHI_1)
    one, zero = jnp.ones((1, 128), jnp.float32), jnp.zeros((1, 128), jnp.float32)
    block_z = [
        jnp.where(element1 < 7, one, jnp.where(element1 == 7, ramp_0, zero)),
        jnp.where(
            element1 == 7,
            ramp_1,
            jnp.where(element1 == 15, ramp_0, jnp.where(element1 > 7, one, zero)),
        ),
        jnp.where(element1 == 15, ramp_1, zero),
    ]
    GROUP = min(16, Q)
    GROUPS = Q // GROUP
    slot_base = 8 * lax.rem(q, GROUP)

    fetches[0].wait()
    started = add_inside(previous[...].reshape(FIELD))

    pl.semaphore_wait(barrier, 8 + (NZ - 1) + (Q - 1))

    send_faces(0, started)
    for fetch in fetches[1:]:
        fetch.wait()

    def far(k, carry):
        pltpu.make_async_remote_copy(
            src_ref=coarse_rows.at[parity, half],
            dst_ref=coarse_rows.at[parity, half],
            send_sem=far_sent,
            recv_sem=far_sems,
            device_id=line_peer(2 * k),
            device_id_type=MESH,
        ).start()
        return carry

    lax.fori_loop(1, NZ // 2, far, 0, unroll=7 if NZ == 16 else 1)

    own_labels = [
        labels[0, 0, 0, 0],
        labels[0, 0, 0, 8],
        labels[1, 0, 0, 15],
        labels[4, 1, 0, 0],
        labels[4, 1, 0, 8],
        labels[5, 1, 0, 15],
    ]
    label_row = jnp.zeros((1, 128), jnp.float32)
    for s in range(6):
        label_row = jnp.where(lane1 == slot_base + s, own_labels[s].astype(jnp.float32), label_row)
    row_send[0] = label_row

    send_rows(0, row_send.at[0], label_rows, q, Q, plane_peer)

    spread_matrix = ((iota((16, 128), 1) >> 3) == iota((16, 128), 0)).astype(jnp.float32)
    spreads = []
    for c in range(3):
        per_x = []
        for a in range(2):
            rows = jnp.dot(
                coefficients[c, a], spread_matrix, precision=HIGHEST, preferred_element_type=jnp.float32
            )
            per_x.append([jnp.broadcast_to(rows[b : b + 1], (8, 128)) for b in range(2)])
        spreads.append(per_x)

    stiff_columns = columns(stiffness, False)
    vector_columns = columns(vectors, False)
    vector_rows = columns(vectors, True)
    stiff_z = block_matrix(columns(stiffness, True))
    forward_z = block_matrix(vector_columns)
    backward_z = block_matrix(vector_rows)

    factor_x = [[spreads[0][a][b] * weight_y * weight_z for b in range(2)] for a in range(2)]
    factor_y = [[spreads[1][a][b] * weight_z for b in range(2)] for a in range(2)]
    factor_z = [[spreads[2][a][b] * weight_y for b in range(2)] for a in range(2)]

    start = masked(over_copies(receive_faces(0, started)))
    start_out[...] = start.reshape(16, 16, 128)
    defect = source[...].reshape(FIELD) - apply_operator(start)
    held = masked(defect)
    flat_x = [held[a, i, 0] + held[a, i, 1] for a in range(2) for i in range(8)]
    sums_x = [
        functools.reduce(jnp.add, flat_x[:8] + [PHI_0[i] * flat_x[8 + i] for i in range(8)]),
        functools.reduce(jnp.add, [PHI_1[i] * flat_x[8 + i] for i in range(8)]),
    ]
    rhs_row = jnp.zeros((1, 128), jnp.float32)
    for a in range(2):
        along = jnp.sum(sums_x[a], axis=0, keepdims=True)
        for b in range(3):
            value = jnp.sum(along * block_z[b], axis=1, keepdims=True)
            rhs_row = jnp.where(lane1 == slot_base + (3 * a + b), value, rhs_row)
    row_send[1] = rhs_row
    send_rows(2, row_send.at[1], rhs_rows, q, Q, plane_peer)

    others = coarse_rows.at[parity, pl.ds(0, NZ // 2 - 1)]

    defect = add_inside(defect)
    send_faces(1, defect)
    pltpu.make_async_copy(others, others, far_sems).wait()
    beside = pltpu.make_async_remote_copy(
        src_ref=coarse_rows.at[parity],
        dst_ref=coarse_rows.at[parity],
        send_sem=near_sems.at[0],
        recv_sem=near_sems.at[1],
        device_id=line_peer(NZ + 1 - 2 * parity),
        device_id_type=MESH,
    )
    beside.start()

    wait_rows(0, label_rows)
    NR = coarse_in.shape[1] // 128
    rows_of = []
    used = (lane1 & 7) < 6
    for g in range(GROUPS):
        packed = jnp.sum(label_rows[pl.ds(g * GROUP, GROUP)], axis=0).astype(jnp.int32)
        packed = jnp.where(used, packed, -1)
        onehot[:, g * 128 : (g + 1) * 128] = jnp.where(iota((128, 128), 0) == (packed & 127), 1.0, 0.0)
        rows_of.append(packed >> 7)

    wait_rows(2, rhs_rows)
    placed = jnp.concatenate(
        [
            jnp.where(
                iota((16, 128), 0) == rows_of[g],
                jnp.sum(rhs_rows[pl.ds(g * GROUP, GROUP)], axis=0),
                0.0,
            )
            for g in range(GROUPS)
        ],
        axis=1,
    )
    rhs = lax.dot_general(
        placed,
        onehot[...],
        (((1,), (1,)), ((), ())),
        precision=HIGHEST,
        preferred_element_type=jnp.float32,
    )
    beside.wait_recv()
    PACK = min(128 // (2 * NZ), Q)
    wide_rows = (NZ // 2, 2, 128)
    line_sum = jnp.zeros((2, 128), jnp.float32)
    for half_line in range(2):
        partial = jnp.zeros(wide_rows, jnp.float32)
        for r in range(NR):
            partial = partial + coarse_rows[half_line, :, :, r * 128 : (r + 1) * 128] * rhs[r : r + 1][None]
        partial = jnp.sum(partial, axis=2, keepdims=True)
        member = 2 * iota(wide_rows, 0) + half_line
        lane_of = lax.rem(q, PACK) * (2 * NZ) + 2 * member + iota(wide_rows, 1)
        line_sum = line_sum + jnp.sum(jnp.where(iota(wide_rows, 2) == lane_of, partial, 0.0), axis=0)
    row_send[2] = jnp.sum(line_sum, axis=0, keepdims=True)
    send_rows(3, row_send.at[2], line_rows, zi, NZ, line_peer)

    residual = masked(receive_faces(1, defect))
    residual_out[...] = residual.reshape(16, 16, 128)
    solved = add_inside(local_solve(residual))
    send_faces(2, solved)

    wait_rows(3, line_rows)
    row_send[3] = jnp.sum(line_rows[...], axis=0)
    send_rows(4, row_send.at[3], value_rows, q, Q, plane_peer)

    local = receive_faces(2, solved)

    wait_rows(4, value_rows)
    value_groups = [jnp.sum(value_rows[pl.ds(g * PACK, PACK)], axis=0) for g in range(Q // PACK)]
    coarse_values = []
    for s in range(6):
        number = jnp.full((1, 128), own_labels[s], jnp.int32)
        bit = number & 1
        device = number >> 1
        label_x, label_z = device // GZ, device % GZ
        row = (label_x // ZL) * YC + label_z % YC
        line = (label_z // YC) * ZL + label_x % ZL
        lane = (row % PACK) * (2 * NZ) + 2 * line + bit
        picked = jnp.zeros((1, 128), jnp.float32)
        for g in range(Q // PACK):
            picked = picked + jnp.where((lane1 == lane) & (row // PACK == g), value_groups[g], 0.0)
        coarse_values.append(jnp.sum(picked, axis=1, keepdims=True))
    first = functools.reduce(jnp.add, [coarse_values[b] * block_z[b] for b in range(3)])
    second = functools.reduce(jnp.add, [coarse_values[3 + b] * block_z[b] for b in range(3)])
    shapes = [[first] * 8, [PHI_0[i] * first + PHI_1[i] * second for i in range(8)]]
    precond = masked(
        join([[[local[a, i, b] + shapes[a][i] for b in range(2)] for i in range(8)] for a in range(2)])
    )
    applied = apply_operator(precond)
    residual = residual_out[...].reshape(FIELD)
    numerator = total(over_copies(residual * precond))
    denominator = total(precond * applied)
    row_send[4] = jnp.where(lane1 == 0, numerator, jnp.where(lane1 == 1, denominator, 0.0))
    send_rows(5, row_send.at[4], sum_rows, q, Q, plane_peer)

    image = add_inside(applied)
    send_faces(3, image)
    wait_rows(5, sum_rows)
    row_send[5] = jnp.sum(sum_rows[...], axis=0)
    send_rows(6, row_send.at[5], total_rows, zi, NZ, line_peer)
    precond_out[...] = precond.reshape(16, 16, 128)
    image_out[...] = masked(receive_faces(3, image)).reshape(16, 16, 128)
    wait_rows(6, total_rows)
    totals = jnp.sum(total_rows[...], axis=0)
    numerator = jnp.sum(jnp.where(lane1 == 0, totals, 0.0), axis=1, keepdims=True)
    denominator = jnp.sum(jnp.where(lane1 == 1, totals, 0.0), axis=1, keepdims=True)
    alpha_out[...] = jnp.broadcast_to(numerator / denominator, (1, 128))

    for n in range(4):
        for s in range(2):
            pltpu.make_async_copy(x_send.at[n, s], x_send.at[n, s], x_sent.at[n, s]).wait()
        for s in range(6):
            pltpu.make_async_copy(z_send.at[n, s], z_send.at[n, s], z_sent.at[n, s]).wait()
    wait_sent(0, label_rows, Q)
    pltpu.make_async_copy(others, others, far_sent).wait()
    beside.wait_send()
    wait_sent(2, rhs_rows, Q)
    wait_sent(3, line_rows, NZ)
    wait_sent(4, value_rows, Q)
    wait_sent(5, sum_rows, Q)
    wait_sent(6, total_rows, NZ)


def split_axes(mesh):
    runs, far = 4, max(2, mesh.shape["gz"] // 16)
    return mesh.shape["gx"] // runs, runs, far, mesh.shape["gz"] // far


def solution(mesh):
    shape = split_axes(mesh)
    XS, ZL, ZH, YC = shape
    Q, NZ = XS * YC, ZL * ZH

    def body(source, previous, coefficients, stiffness, vectors, eigen, coarse, labels):
        f32 = jnp.float32
        field = pltpu.VMEM(source.shape, f32)
        operands = (source, previous, coefficients, stiffness, vectors, eigen, coarse, labels)
        start, precond, residual, image, alpha = pl.pallas_call(
            functools.partial(tile_kernel, shape),
            out_shape=(field, field, field, field, pltpu.VMEM((1, 128), f32)),
            in_specs=[pl.BlockSpec(memory_space=pl.ANY)] * 8,
            out_specs=(pl.BlockSpec(memory_space=pltpu.VMEM),) * 5,
            scratch_shapes=[
                pltpu.VMEM(source.shape, f32),
                pltpu.VMEM(source.shape, f32),
                pltpu.VMEM(coefficients.shape, f32),
                pltpu.SMEM(stiffness.shape, f32),
                pltpu.SMEM(vectors.shape, f32),
                pltpu.SMEM(eigen.shape, f32),
                pltpu.SMEM(labels.shape, jnp.int32),
                pltpu.VMEM((4, 2, 16, 128), f32),
                pltpu.VMEM((4, 2, 16, 128), f32),
                pltpu.VMEM((4, 6, 1, 256), f32),
                pltpu.VMEM((4, 6, 1, 256), f32),
                pltpu.VMEM((6, 1, 128), f32),
                pltpu.VMEM((Q, 1, 128), f32),
                pltpu.VMEM((Q, 1, 128), f32),
                pltpu.VMEM((NZ, 1, 128), f32),
                pltpu.VMEM((Q, 1, 128), f32),
                pltpu.VMEM((Q, 1, 128), f32),
                pltpu.VMEM((NZ, 1, 128), f32),
                pltpu.VMEM((2, NZ // 2, 2, coarse.shape[1]), f32),
                pltpu.VMEM((128, 128 * max(1, Q // 16)), f32),
                pltpu.SemaphoreType.DMA((4, 2)),
                pltpu.SemaphoreType.DMA((4, 6)),
                pltpu.SemaphoreType.DMA((4, 2)),
                pltpu.SemaphoreType.DMA((4, 6)),
                pltpu.SemaphoreType.DMA((7,)),
                pltpu.SemaphoreType.DMA((7,)),
                pltpu.SemaphoreType.DMA,
                pltpu.SemaphoreType.DMA,
                pltpu.SemaphoreType.DMA((2,)),
                pltpu.SemaphoreType.DMA((8,)),
            ],
            compiler_params=pltpu.CompilerParams(collective_id=0, has_side_effects=True),
        )(*operands)
        alpha = alpha[None]
        return start + alpha * precond, residual - alpha * image

    placed = (
        P("gx", None, "gz"),
        P("gx", None, "gz"),
        P(None, "gx", None, "gz"),
        P(),
        P(),
        P(),
        P(("gx", "gz"), None),
        P(None, "gx", None, "gz"),
    )
    return jax.shard_map(
        body,
        mesh=mesh,
        in_specs=placed,
        out_specs=(P("gx", None, "gz"), P("gx", None, "gz")),
        check_vma=False,
    )
```
